512 devices in a mesh: sect: 8 (over z), wide: 16 (over y, core), narrow: 4 (over x).
Axes of the slice: x: 4, y: 8, z: 8, core: 2. Of those that a mesh axis runs over, the one named last changes fastest.
Arguments:
- leaf_rhs: bfloat16 [512, 32768], P('wide', ('sect', 'narrow')), may hold values from -6 to 6
- leaf_factor: bfloat16 [32768, 4096], P(('sect', 'wide'), 'narrow'), may hold values from -1 to 2
- leaf_coupling: bfloat16 [16384, 4096], P(('sect', 'wide'), 'narrow'), may hold values from -0.09375 to 0.09375
- root_factor: bfloat16 [16384, 16384], P('wide', ('sect', 'narrow')), may hold values from -1 to 2
- root_rhs: bfloat16 [512, 16384], P('wide', ('sect', 'narrow')), may hold values from -6 to 6
- border_map: int32 [8, 2048], replicated, may hold values from 0 to 16383, as said below
- border_rows: int32 [8], replicated, may hold values from 512 to 2048, as said below
Outputs:
- leaf_solution: bfloat16 [512, 32768], P('wide', ('sect', 'narrow'))
- root_solution: bfloat16 [512, 16384], P('wide', ('sect', 'narrow'))
The draws below stay inside these ranges and needn't reach their ends.
Inputs may be any that keep to these rules, and one draw needn't show every extreme that they name: `border_map`: row s lists the root indices of the 2048 border rows of leaf s, all different within a row; different leaves may share root indices. The live border rows of leaf s are its first border_rows[s] rows.
All inputs are finite; a program needn't handle non-finite values.
Results may differ from the reference program's by a relative error of at most 0.024.
Values may be sent and summed in bfloat16 or wider, within the bound.
A program may use at most 64 MiB of HBM per device.

```python
import math
import jax
import jax.numpy as jnp
from jax import lax

RHS = 512
PIVOTS = 4096
BORDER = 2048
ROOT = 16384
LEAVES = 8
LEAF_SPLIT = 4
ROOT_SPLIT = 32
ROW_SPLIT = 16


def factor_draw(key, rows, columns):
    spread_key, diagonal_key = jax.random.split(key)
    spread = jnp.clip(jax.random.normal(spread_key, (rows, columns), jnp.float32), -5.0, 5.0) * (0.4 / math.sqrt(columns))
    diagonal = jax.random.uniform(diagonal_key, (rows, 1), jnp.float32, 0.6, 1.4)
    row_place = lax.broadcasted_iota(jnp.int32, (rows, columns), 0) % columns
    column_place = lax.broadcasted_iota(jnp.int32, (rows, columns), 1)
    return (spread + jnp.where(row_place == column_place, diagonal, 0.0)).astype(jnp.bfloat16)


def draw_leaf_factor(key, part):
    return factor_draw(jax.random.fold_in(key, 11), LEAVES * PIVOTS, PIVOTS)


def draw_root_factor(key, part):
    return factor_draw(jax.random.fold_in(key, 13), ROOT, ROOT)


def draw_border_map(key, part):
    leaf_keys = jax.random.split(jax.random.fold_in(key, 17), LEAVES)

    def one_leaf(leaf_key):
        order = jax.random.permutation(leaf_key, ROOT).astype(jnp.int32)
        order = (order + (ROOT - 1 - order[0])) % ROOT
        return order[:BORDER]
    return jax.vmap(one_leaf)(leaf_keys).astype(jnp.int32)


def draw_border_rows(key, part):
    count_key, full_key = jax.random.split(jax.random.fold_in(key, 19))
    counts = jax.random.randint(count_key, (LEAVES,), BORDER // 4, BORDER + 1, jnp.int32)
    chosen = jax.random.randint(full_key, (), 0, LEAVES, jnp.int32)
    places = lax.broadcasted_iota(jnp.int32, (LEAVES,), 0)
    return jnp.where(places == chosen, BORDER, counts).astype(jnp.int32)


def levels(own_key, shape, cuts, least, largest):
    def one(dim, shards_of):
        heights = jax.random.uniform(jax.random.fold_in(jax.random.fold_in(own_key, 6), dim), (shards_of,), jnp.float32, least / len(cuts), largest / len(cuts))
        return jnp.repeat(jnp.exp(heights), shape[dim] // shards_of).reshape((-1,) + (1,) * (len(shape) - dim - 1))

    factor_of = one(*cuts[0])
    for cut in cuts[1:]:
        factor_of = factor_of * one(*cut)
    return factor_of


def bell_draw(stream_key, shape, deviation, reach, cuts=(), kind=jnp.bfloat16):
    array = jax.random.normal(stream_key, shape, jnp.float32) * deviation
    if len(cuts) > 0:
        array = levels(stream_key, shape, cuts, -0.22, 0.18) * array
    return jnp.clip(array, min=-reach, max=reach).astype(kind)


def setup_inputs(seed: int = 0) -> dict:
    streams_of = jax.random.split(jax.random.key(seed), 8)
    return {
        "leaf_rhs": bell_draw(streams_of[0], (RHS, LEAVES * PIVOTS), 1.0, 6.0, ((0, 16), (1, 32))),
        "leaf_factor": draw_leaf_factor(jax.random.fold_in(streams_of[7], 71), 0),
        "leaf_coupling": bell_draw(streams_of[2], (LEAVES * BORDER, PIVOTS), PIVOTS ** -0.5, 0.09375, ((0, 128), (1, 4))),
        "root_factor": draw_root_factor(jax.random.fold_in(streams_of[7], 71), 0),
        "root_rhs": bell_draw(streams_of[4], (RHS, ROOT), 1.0, 6.0, ((0, 16), (1, 32))),
        "border_map": draw_border_map(jax.random.fold_in(streams_of[7], 71), 0),
        "border_rows": draw_border_rows(jax.random.fold_in(streams_of[7], 71), 0),
    }


def rounded(value):
    return lax.optimization_barrier(value.astype(jnp.bfloat16)).astype(jnp.float32)


def times_transposed(left, right):
    return lax.dot_general(left, right, (((1,), (1,)), ((), ())), preferred_element_type=jnp.float32)


def reference(leaf_rhs, leaf_factor, leaf_coupling, root_factor, root_rhs, border_map, border_rows):
    column_width = PIVOTS // LEAF_SPLIT
    border_place = lax.broadcasted_iota(jnp.int32, (1, BORDER), 1)
    leaf_mids = []
    border_parts = []
    for leaf_index in range(LEAVES):
        rhs_leaf = leaf_rhs[:, leaf_index * PIVOTS:(leaf_index + 1) * PIVOTS]
        factor = leaf_factor[leaf_index * PIVOTS:(leaf_index + 1) * PIVOTS]
        coupling = leaf_coupling[leaf_index * BORDER:(leaf_index + 1) * BORDER]
        stacked = jnp.concatenate([factor, coupling], axis=0)
        summed = jnp.zeros((RHS, PIVOTS + BORDER), jnp.float32)
        for block in range(LEAF_SPLIT):
            columns = slice(block * column_width, (block + 1) * column_width)
            summed = summed + rounded(times_transposed(rhs_leaf[:, columns], stacked[:, columns]))
        leaf_mids.append(summed[:, :PIVOTS].astype(jnp.bfloat16))
        active = border_place < border_rows[leaf_index]
        border_parts.append(jnp.where(active, summed[:, PIVOTS:], jnp.float32(0.0)).astype(jnp.bfloat16))
    extend = jnp.zeros((RHS, ROOT), jnp.float32)
    for leaf_index in range(LEAVES):
        extend = extend.at[:, border_map[leaf_index]].add(border_parts[leaf_index].astype(jnp.float32))
    root_right = (root_rhs.astype(jnp.float32) - extend).astype(jnp.bfloat16)

    root_width = ROOT // ROOT_SPLIT

    def forward_block(block, summed):
        right_columns = lax.dynamic_slice_in_dim(root_right, block * root_width, root_width, 1)
        factor_columns = lax.dynamic_slice_in_dim(root_factor, block * root_width, root_width, 1)
        return summed + rounded(times_transposed(right_columns, factor_columns))

    root_mid = lax.fori_loop(0, ROOT_SPLIT, forward_block, jnp.zeros((RHS, ROOT), jnp.float32)).astype(jnp.bfloat16)

    row_width = ROOT // ROW_SPLIT

    def back_block(block, summed):
        mid_columns = lax.dynamic_slice_in_dim(root_mid, block * row_width, row_width, 1)
        factor_rows = lax.dynamic_slice_in_dim(root_factor, block * row_width, row_width, 0)
        return summed + rounded(jnp.dot(mid_columns, factor_rows, preferred_element_type=jnp.float32))

    root_solution = lax.fori_loop(0, ROW_SPLIT, back_block, jnp.zeros((RHS, ROOT), jnp.float32)).astype(jnp.bfloat16)

    pivot_width = PIVOTS // ROW_SPLIT
    border_width = BORDER // ROW_SPLIT
    solutions = []
    for leaf_index in range(LEAVES):
        factor = leaf_factor[leaf_index * PIVOTS:(leaf_index + 1) * PIVOTS]
        coupling = leaf_coupling[leaf_index * BORDER:(leaf_index + 1) * BORDER]
        active = border_place < border_rows[leaf_index]
        returned = jnp.where(active, root_solution[:, border_map[leaf_index]], jnp.zeros((), jnp.bfloat16))
        summed = jnp.zeros((RHS, PIVOTS), jnp.float32)
        for block in range(ROW_SPLIT):
            pivot_span = slice(block * pivot_width, (block + 1) * pivot_width)
            border_span = slice(block * border_width, (block + 1) * border_width)
            difference = jnp.dot(leaf_mids[leaf_index][:, pivot_span], factor[pivot_span], preferred_element_type=jnp.float32)
            difference = difference - jnp.dot(returned[:, border_span], coupling[border_span], preferred_element_type=jnp.float32)
            summed = summed + rounded(difference)
        solutions.append(summed.astype(jnp.bfloat16))
    leaf_solution = jnp.concatenate(solutions, axis=1)
    return leaf_solution, root_solution
```

```python
import functools

import jax
import jax.numpy as jnp
from jax import lax
from jax.experimental import pallas as pl
from jax.experimental.pallas import tpu as pltpu
from jax.sharding import PartitionSpec as P

MESH = pl.DeviceIdType.MESH
F32 = jnp.float32
BF16 = jnp.bfloat16
SEMS = 320
STOP = 99


class Stop(Exception):
    pass


def nt(a, b):
    return lax.dot_general(a, b, (((1,), (1,)), ((), ())), preferred_element_type=F32)


def nn(a, b):
    return jnp.dot(a, b, preferred_element_type=F32)


class Wire:
    def __init__(self, send, recv):
        self.send, self.recv, self.used, self.started, self.open = send, recv, 0, [], []

    def copy(self, src, dst, **device):
        k = self.used
        self.used += 1
        assert k < SEMS
        c = pltpu.make_async_remote_copy(
            src_ref=src, dst_ref=dst, send_sem=self.send.at[k], recv_sem=self.recv.at[k],
            device_id=device, device_id_type=MESH,
        )
        c.start()
        self.started.append(c)
        self.open.append(c)
        return c

    def got(self, *copies):
        for c in copies:
            c.wait_recv()
            self.open = [o for o in self.open if o is not c]

    def finish(self):
        for c in list(self.open):
            self.got(c)
        for c in self.started:
            c.wait_send()


def kernel(stop, lr, G, W, F, rr, bmap, brows, leaf_out, root_out,
           X1, SB, RB, PB, RP, YB, U, Z, LT, A, SL, RL, RR,
           YP, RX1, RXO, SX2, RX2, Q1, RZ, MID,
           B2, S2, A2, D2, SX, T, AX, XW, Q,
           B3, S3, A3, V3, D3, HM, send, recv):
    s = lax.axis_index("sect")
    w = lax.axis_index("wide")
    n = lax.axis_index("narrow")
    y = w // 2
    c = lax.rem(w, 2)
    oc = 1 - c
    wire = Wire(send, recv)

    def zs(j):
        return lax.rem(s + j, 8)

    def ys(j):
        return lax.rem(y + j, 8)

    def xs(j):
        return lax.rem(n + j, 4)

    def rows(start, size):
        return pl.ds(pl.multiple_of(start, size), size)

    barrier = pltpu.get_barrier_semaphore()
    for j in range(1, 16):
        pl.semaphore_signal(barrier, inc=1, device_id={"wide": lax.rem(w + j, 16)}, device_id_type=MESH)
    for j in range(1, 4):
        pl.semaphore_signal(barrier, inc=1, device_id={"narrow": xs(j)}, device_id_type=MESH)
    for j in range(1, 8):
        pl.semaphore_signal(barrier, inc=1, device_id={"sect": zs(j)}, device_id_type=MESH)
    X1[w] = lr[...]
    pl.semaphore_wait(barrier, 25)

    def gather_ring(buf):
        half = (pl.ds(0, 16), pl.ds(16, 16))
        deep = {(1, 0): 4, (1, 1): 3, (-1, 0): 3, (-1, 1): 4}
        pair, moving = [], {}
        for h in range(2):
            for d in (1, -1):
                ref = buf.at[w, half[h]]
                moving[d, h] = wire.copy(ref, ref, wide=2 * ys(d % 8) + c)
        pair.append(wire.copy(buf.at[w], buf.at[w], wide=2 * y + oc))
        for k in range(1, 5):
            for h in range(2):
                for d in (1, -1):
                    if k > deep[d, h]:
                        continue
                    wire.got(moving[d, h])
                    ref = buf.at[2 * ys(-d * k % 8) + c, half[h]]
                    if k < deep[d, h]:
                        moving[d, h] = wire.copy(ref, ref, wide=2 * ys(d % 8) + c)
                    pair.append(wire.copy(ref, ref, wide=2 * y + oc))
        wire.got(*pair)

    def gather_direct(buf):
        order = (1, 7, 2, 6, 3, 5, 4)
        pair = []
        out = [wire.copy(buf.at[w], buf.at[w], wide=2 * ys(j) + c) for j in order]
        pair.append(wire.copy(buf.at[w], buf.at[w], wide=2 * y + oc))
        for j, got in zip(order, out):
            wire.got(got)
            ref = buf.at[2 * ys(-j % 8) + c]
            pair.append(wire.copy(ref, ref, wide=2 * y + oc))
        wire.got(*pair)

    def pair_sum(B, S, acc):
        wire.got(wire.copy(B.at[oc], S, wide=2 * y + oc))
        acc[...] = (B[c].astype(F32) + S[...].astype(F32)).astype(BF16)

    def scatter_direct(B, S, acc, D):
        pair_sum(B, S, acc)
        order = (4, 3, 5, 2, 6, 1, 7)
        out = [wire.copy(acc.at[ys(j)], D.at[j - 1], wide=2 * ys(j) + c) for j in order]
        wire.got(*out)
        total = acc[y].astype(F32)
        for j in range(7):
            total = total + D[j].astype(F32)
        return total

    def scatter_ring(B, S, acc, V, D):
        pair_sum(B, S, acc)
        half = (pl.ds(0, 16), pl.ds(16, 16))
        deep = {(1, 0): 4, (1, 1): 3, (-1, 0): 3, (-1, 1): 4}
        lane = {(1, 0): 0, (1, 1): 1, (-1, 0): 2, (-1, 1): 3}
        moving = {}
        for k in range(4, -1, -1):
            for h in range(2):
                for d in (1, -1):
                    i = lane[d, h]
                    if k > deep[d, h]:
                        continue
                    if k == deep[d, h]:
                        src = acc.at[ys(d * k % 8), half[h]]
                        moving[d, h] = wire.copy(src, D.at[i, k - 1], wide=2 * ys(d % 8) + c)
                        continue
                    wire.got(moving[d, h])
                    if k >= 1:
                        V[i, k - 1] = (acc[ys(d * k % 8), half[h]].astype(F32) + D[i, k].astype(F32)).astype(BF16)
                        moving[d, h] = wire.copy(V.at[i, k - 1], D.at[i, k - 1], wide=2 * ys(d % 8) + c)
        return [acc[y, half[h]].astype(F32) + D[lane[1, h], 0].astype(F32) + D[lane[-1, h], 0].astype(F32)
                for h in range(2)]

    def at(phase):
        if phase > stop:
            raise Stop

    try:
        place = lax.broadcasted_iota(jnp.int32, (128, 128), 0)
        for leaf in range(8):
            for i in range(16):
                HM[leaf, i] = jnp.broadcast_to(bmap[pl.ds(leaf, 1), pl.ds(128 * i, 128)], (8, 128))

        def low(leaf, _):
            for i in range(16):
                span = pl.ds(i * 128, 128)
                value = jnp.concatenate([HM[leaf, i] & 127] * 16, axis=0)
                LT[leaf, :, span] = jnp.where(place == value, 1.0, 0.0).astype(BF16)
            return 0

        lax.fori_loop(0, 8, low, 0)
        gather_ring(X1)

        at(1)
        for b in range(4):
            block = X1[pl.ds(4 * b, 4)].reshape(128, 1024)
            t = nt(block, W[...]).reshape(4, 4, 8, 128)
            for i in range(4):
                SB[i, pl.ds(4 * b, 4)] = t[:, i].astype(BF16)
        sums = [wire.copy(SB.at[xs(j)], RB.at[j - 1], narrow=xs(j)) for j in (2, 1, 3)]
        for b in range(4):
            block = X1[pl.ds(4 * b, 4)].reshape(128, 1024)
            PB[b] = nt(block, G[...]).astype(BF16)
        pivots = [wire.copy(PB.at[xs(j)], RP.at[j - 1], narrow=xs(j)) for j in (2, 1, 3)]
        wire.got(*sums)
        total = SB[n].astype(F32)
        for j in range(3):
            total = total + RB[j].astype(F32)
        live = lax.broadcasted_iota(jnp.int32, (16, 8, 128), 2) + w * 128 < brows[s]
        U[...] = jnp.where(live, total, 0.0).astype(BF16)

        at(2)
        parts = [wire.copy(U.at[lax.rem(w + j, 16)], Z.at[s, w], wide=lax.rem(w + j, 16)) for j in range(1, 16)]
        Z[s, w] = U[w]
        wire.got(*parts)

        at(3)
        spread = [wire.copy(Z.at[s], Z.at[s], sect=zs(j)) for j in (4, 3, 5, 2, 6, 1, 7)]
        wire.got(*pivots)
        total = PB[n].astype(F32)
        for j in range(3):
            total = total + RP[j].astype(F32)
        YB[n] = total.astype(BF16)
        mids = [wire.copy(YB.at[n], YB.at[n], narrow=xs(j)) for j in (2, 1, 3)]
        wire.got(*spread)

        at(4)

        def add_leaf(leaf, landed):
            for i in range(16):
                span = pl.ds(i * 128, 128)
                high = (HM[leaf, i] - s * 2048) >> 7
                value = Z[leaf, i].astype(F32)
                A[:, span] = jnp.concatenate(
                    [jnp.where(high == h, value, 0.0) for h in range(16)], axis=0
                ).astype(BF16)
            return landed + nt(A[...], LT[leaf])

        landed = lax.fori_loop(0, 8, add_leaf, jnp.zeros((128, 128), F32))
        SL[...] = landed.reshape(4, 4, 8, 128)

        at(5)
        out = [wire.copy(SL.at[xs(j)], RL.at[n], narrow=xs(j)) for j in (2, 1, 3)]
        RL[n] = SL[n]
        wire.got(*out)
        for i in range(4):
            right = rr[:, pl.ds(128 * i, 128)].astype(F32)
            put = jnp.concatenate([RL[k, i] for k in range(4)], axis=0)
            RR[w, :, pl.ds(128 * i, 128)] = (right - put).astype(BF16)

        at(6)
        gather_direct(RR)

        at(7)
        def forward(q):
            YP[q] = nt(RR[pl.ds(4 * q, 4)].reshape(128, 512), F[...]).astype(BF16)

        up, down, far = xs(1), xs(3), xs(2)
        h0, h1 = pl.ds(0, 64), pl.ds(64, 64)
        forward(far)
        a0 = wire.copy(YP.at[far, h0], RX1.at[0], narrow=up)
        a1 = wire.copy(YP.at[far, h1], RX1.at[1], narrow=down)
        forward(up)
        o0 = wire.copy(YP.at[up, h1], RXO.at[0], narrow=up)
        forward(down)
        o1 = wire.copy(YP.at[down, h0], RXO.at[1], narrow=down)
        wire.got(a0)
        SX2[0] = (YP[up, h0].astype(F32) + RX1[0].astype(F32)).astype(BF16)
        b0 = wire.copy(SX2.at[0], RX2.at[0], narrow=up)
        wire.got(a1)
        SX2[1] = (YP[down, h1].astype(F32) + RX1[1].astype(F32)).astype(BF16)
        b1 = wire.copy(SX2.at[1], RX2.at[1], narrow=down)
        forward(n)
        wire.got(o0, o1, b0, b1)
        Q1[h0] = (YP[n, h0].astype(F32) + RX2[0].astype(F32) + RXO[1].astype(F32)).astype(BF16)
        Q1[h1] = (YP[n, h1].astype(F32) + RX2[1].astype(F32) + RXO[0].astype(F32)).astype(BF16)

        at(8)
        out = [wire.copy(Q1.at[rows(16 * zs(j), 16)], RZ.at[j - 1], sect=zs(j)) for j in (4, 3, 5, 2, 6, 1, 7)]
        wire.got(*out)
        mine = rows(16 * s, 16)
        total = Q1[mine].astype(F32)
        for j in range(7):
            total = total + RZ[j].astype(F32)
        MID[n, mine] = total.astype(BF16)

        at(9)
        ref = MID.at[n, mine]
        wire.got(*[wire.copy(ref, ref, sect=zs(j)) for j in (4, 3, 5, 2, 6, 1, 7)])

        at(10)
        def half(q, h):
            return MID.at[q, h]

        p0 = wire.copy(half(n, h0), half(n, h0), narrow=up)
        m1 = wire.copy(half(n, h1), half(n, h1), narrow=down)
        p1 = wire.copy(half(n, h1), half(n, h1), narrow=up)
        m0 = wire.copy(half(n, h0), half(n, h0), narrow=down)

        def backward(q):
            t = nn(MID[q], F[...]).astype(BF16)
            for i in range(4):
                B2[i % 2, 2 * q + i // 2] = t[32 * i:32 * i + 32]

        backward(n)
        wire.got(p0)
        f0 = wire.copy(half(down, h0), half(down, h0), narrow=up)
        wire.got(m1)
        f1 = wire.copy(half(up, h1), half(up, h1), narrow=down)
        wire.got(p1)
        backward(down)
        wire.got(m0)
        backward(up)
        wire.got(f0, f1)
        backward(far)

        at(11)
        total = scatter_direct(B2, S2, A2, D2)
        root_out[...] = total.astype(BF16)
        for i in range(4):
            for k in range(4):
                SX[i, k] = total[8 * i:8 * i + 8, 128 * k:128 * k + 128].astype(BF16)

        at(12)
        slot = rows(4 * n, 4)
        out = [wire.copy(SX.at[xs(j)], T.at[s, slot], narrow=xs(j)) for j in (2, 1, 3)]
        T[s, slot] = SX[n]
        wire.got(*out)

        at(13)
        wire.got(*[wire.copy(T.at[s], T.at[s], sect=zs(j)) for j in (4, 3, 5, 2, 6, 1, 7)])

        at(14)
        for i in range(8):
            for k in range(16):
                AX[i, pl.ds(8 * k, 8)] = T[i, k].astype(F32)

        def pick(i, _):
            span = pl.ds(pl.multiple_of(128 * i, 128), 128)
            live = lax.broadcasted_iota(jnp.int32, (8, 128), 1) + i * 128 < brows[s]
            high = jnp.where(live, HM[s, i] >> 7, -1)
            found = jnp.zeros((8, 128), F32)
            for g in range(8):
                t = nn(AX[g].astype(BF16), LT[s, :, span])
                for k in range(16):
                    found = found + jnp.where(high == 16 * g + k, t[8 * k:8 * k + 8], 0.0)
            XW[i] = found.astype(BF16)
            return 0

        lax.fori_loop(0, 16, pick, 0)

        at(15)
        out = [wire.copy(XW.at[lax.rem(w + j, 16)], Q.at[n, w], wide=lax.rem(w + j, 16)) for j in range(1, 16)]
        Q[n, w] = XW[w]
        wire.got(*out)
        wire.got(*[wire.copy(Q.at[n], Q.at[n], narrow=xs(j)) for j in (2, 1, 3)])
        wire.got(*mids)

        at(16)
        for b in range(4):
            x2 = jnp.concatenate(
                [Q[k, 4 * b + i].astype(F32) for i in range(4) for k in range(4)], axis=0
            ).astype(BF16)
            t = (nn(YB[b], G[...]) - nn(x2, W[...])).astype(BF16)
            for i in range(4):
                B3[i % 2, 2 * b + i // 2] = t[32 * i:32 * i + 32]

        at(17)
        top, bottom = scatter_ring(B3, S3, A3, V3, D3)
        leaf_out[pl.ds(0, 16)] = top.astype(BF16)
        leaf_out[pl.ds(16, 16)] = bottom.astype(BF16)
    except Stop:
        pass
    wire.finish()


def body(leaf_rhs, leaf_factor, leaf_coupling, root_factor, root_rhs, border_map, border_rows, stop=STOP):
    vmem = pl.BlockSpec(memory_space=pltpu.VMEM)
    smem = pl.BlockSpec(memory_space=pltpu.SMEM)

    def bf(*shape):
        return pltpu.VMEM(shape, BF16)

    def fl(*shape):
        return pltpu.VMEM(shape, F32)

    scratch = [
        bf(16, 32, 1024), bf(4, 16, 8, 128), bf(3, 16, 8, 128), bf(4, 128, 256), bf(3, 128, 256), bf(4, 128, 256),
        bf(16, 8, 128), bf(8, 16, 8, 128), bf(8, 128, 2048), bf(128, 2048), fl(4, 4, 8, 128), fl(4, 4, 8, 128),
        bf(16, 32, 512),
        bf(4, 128, 1024), bf(2, 64, 1024), bf(2, 64, 1024), bf(2, 64, 1024), bf(2, 64, 1024), bf(128, 1024),
        bf(7, 16, 1024), bf(4, 128, 1024),
        bf(2, 8, 32, 512), bf(8, 32, 512), bf(8, 32, 512), bf(7, 32, 512), bf(4, 4, 8, 128), bf(8, 16, 8, 128),
        fl(8, 128, 128), bf(16, 8, 128), bf(4, 16, 8, 128),
        bf(2, 8, 32, 1024), bf(8, 32, 1024), bf(8, 32, 1024), bf(4, 4, 16, 1024), bf(4, 4, 16, 1024),
        pltpu.VMEM((8, 16, 8, 128), jnp.int32),
        pltpu.SemaphoreType.DMA((SEMS,)), pltpu.SemaphoreType.DMA((SEMS,)),
    ]
    return pl.pallas_call(
        functools.partial(kernel, stop),
        out_shape=(
            jax.ShapeDtypeStruct((32, 1024), BF16),
            jax.ShapeDtypeStruct((32, 512), BF16),
        ),
        in_specs=[vmem] * 6 + [smem],
        out_specs=(vmem, vmem),
        scratch_shapes=scratch,
        compiler_params=pltpu.CompilerParams(
            collective_id=0, has_side_effects=True, vmem_limit_bytes=60000 * 1024
        ),
    )(leaf_rhs, leaf_factor, leaf_coupling, root_factor, root_rhs, border_map, border_rows)


def solution(mesh, stop=STOP):
    in_specs = (
        P("wide", ("sect", "narrow")),
        P(("sect", "wide"), "narrow"),
        P(("sect", "wide"), "narrow"),
        P("wide", ("sect", "narrow")),
        P("wide", ("sect", "narrow")),
        P(),
        P(),
    )
    out_specs = (P("wide", ("sect", "narrow")), P("wide", ("sect", "narrow")))
    return jax.shard_map(
        functools.partial(body, stop=stop), mesh=mesh, in_specs=in_specs, out_specs=out_specs, check_vma=False
    )
```
